128 devices in a mesh: tm: 4 (over z_hi, core), pair: 32 (over z_lo, y, x).
Axes of the slice: x: 4, y: 4, z: 4 (z_hi: 2, z_lo: 2; z = z_hi * 2 + z_lo), core: 2. Of those that a mesh axis runs over, the one named last changes fastest.
Arguments:
- orbitals: bfloat16 [32768, 512], P('pair', 'tm'), may hold values from -1.5 to 1.5
- level_gap: float32 [512], replicated, may hold values from 0.05 to 1.5
- screened: bfloat16 [8, 128, 1024, 1024], P('tm', 'pair'), may hold values from -0.008972168 to 0.008972168
- pair_blocks: int32 [128, 2], P('pair'), may hold values from 0 to 31, as said below
Outputs:
- self_energy: float32 [8, 512, 512], P('tm', 'pair')
The draws below stay inside these ranges and needn't reach their ends.
Inputs may be any that keep to these rules, and one draw needn't show every extreme that they name: `pair_blocks`: each row names two point blocks a <= c; no unordered pair appears in two rows; the pair (0, 31) appears in every draw.
All inputs are finite; a program needn't handle non-finite values.
Results may differ from the reference program's by a relative error of at most 0.0049.
Values may be sent and summed in bfloat16 or wider, within the bound.
No kernel may reach another device: no remote copies, remote signals or barrier semaphores. Data moves between devices by JAX's collectives and lax.ppermute only.
A program may use at most 128 MiB of HBM per device.

```python
import math
import jax
import jax.numpy as jnp
from jax import lax

NORB = 512
NOCC = 128
BLK = 1024
NT = 8
PAIRS = 128
NPTS = 32768
N_PAIR = 32


def draw_pair_blocks(key, part):
    count = N_PAIR * N_PAIR
    flat = jnp.arange(count, dtype=jnp.int32)
    first = flat // N_PAIR
    second = flat % N_PAIR
    ranks = jax.random.permutation(jax.random.fold_in(key, 11), count).astype(jnp.int32)
    ranks = jnp.where(first <= second, ranks, ranks + count)
    ranks = jnp.where((first == 0) & (second == N_PAIR - 1), jnp.int32(-1), ranks)
    order = jnp.argsort(ranks, stable=True)[:PAIRS]
    shuffle = jax.random.permutation(jax.random.fold_in(key, 23), PAIRS)
    picked = order[shuffle]
    return jnp.stack([first[picked], second[picked]], axis=1).astype(jnp.int32)


def block_levels(own_key, extent, split, least, largest):
    def one(dim, shards_of):
        steps = jax.random.uniform(jax.random.fold_in(jax.random.fold_in(own_key, 6), dim), (shards_of,), jnp.float32, least / len(split), largest / len(split))
        return jnp.repeat(jnp.exp(steps), extent[dim] // shards_of).reshape((-1,) + (1,) * (len(extent) - dim - 1))

    level = one(*split[0])
    for cut in split[1:]:
        level = level * one(*cut)
    return level


def scatter_about(stream_key, extent, scale, limit, pieces=(), held_as=jnp.bfloat16):
    entries = scale * jax.random.normal(stream_key, extent, jnp.float32)
    if pieces:
        entries = entries * block_levels(stream_key, extent, pieces, -0.22, 0.18)
    return jnp.clip(entries, -limit, limit).astype(held_as)


def setup_inputs(seed: int = 0) -> dict:
    keys = jax.random.split(jax.random.key(seed), 5)
    return {
        "orbitals": scatter_about(keys[0], (NPTS, NORB), 0.25, 1.5, ((0, 32), (1, 4))),
        "level_gap": jnp.clip(jnp.exp(jax.random.uniform(keys[1], (NORB,), jnp.float32, math.log(0.05), math.log(1.5))), 0.05, 1.5),
        "screened": scatter_about(keys[2], (NT, PAIRS, BLK, BLK), 0.0015, 0.008972168, ((0, 4), (1, 32))),
        "pair_blocks": draw_pair_blocks(jax.random.fold_in(keys[4], 71), 0),
    }


def reference(orbitals, level_gap, screened, pair_blocks):
    blocks = orbitals.reshape(NPTS // BLK, BLK, NORB)
    tau = 6.0 * (jnp.arange(NT, dtype=jnp.float32) + 0.5) / NT
    signs = jnp.where(jnp.arange(NORB) < NOCC, 1.0, -1.0).astype(jnp.float32)
    factors = signs[None, :] * jnp.exp(-level_gap[None, :] * tau[:, None])

    def per_time(items):
        factor, tiles = items

        def step(total, item):
            tile, pair = item
            left = blocks[pair[0]]
            right = blocks[pair[1]]
            scaled = (left.astype(jnp.float32) * factor[None, :]).astype(jnp.bfloat16)
            green = lax.dot_general(scaled, right, (((1,), (1,)), ((), ())), preferred_element_type=jnp.float32)
            product = (green * tile.astype(jnp.float32)).astype(jnp.bfloat16)
            half = lax.dot_general(left, product, (((0,), (0,)), ((), ())), preferred_element_type=jnp.float32).astype(jnp.bfloat16)
            block = jnp.dot(half, right, preferred_element_type=jnp.float32)
            weight = jnp.where(pair[0] == pair[1], 0.5, 1.0).astype(jnp.float32)
            return total + weight * (block + block.T), None

        total, unused = lax.scan(step, jnp.zeros((NORB, NORB), jnp.float32), (tiles, pair_blocks))
        return total

    return lax.map(per_time, (factors, screened))
```

```python
import jax
import jax.numpy as jnp
from jax import lax
from jax.experimental import pallas as pl
from jax.experimental.pallas import tpu as pltpu
from jax.sharding import Mesh
from jax.sharding import PartitionSpec as P

NOCC = 128
PAIR = ("zl", "y", "x")
SAME_CORE = ("zh", "zl", "y", "x")
CHUNKS = ((0, 2), (2, 2))
INDEX_ROWS = 8


def picked_for(wants, slices, first, count):
    owners, rows, cols = slices.shape[0], slices.shape[1] - INDEX_ROWS, slices.shape[2]
    per_step = 8

    def kernel(wants_ref, slices_ref, out_ref):
        step = pl.program_id(1)
        for d in range(per_step):
            for k in range(count):
                block = wants_ref[step * per_step + d, first + k]
                out_ref[0, d, k] = slices_ref[block, :rows, :]

    return pl.pallas_call(
        kernel,
        grid_spec=pltpu.PrefetchScalarGridSpec(
            num_scalar_prefetch=1,
            grid=(2, owners // per_step),
            in_specs=[pl.BlockSpec(slices.shape, lambda h, i, w: (0, 0, 0))],
            out_specs=pl.BlockSpec((1, per_step, count, rows, cols), lambda h, i, w: (h, i, 0, 0, 0)),
        ),
        out_shape=jax.ShapeDtypeStruct((2, owners, count, rows, cols), slices.dtype),
        compiler_params=pltpu.CompilerParams(dimension_semantics=("arbitrary", "arbitrary")),
    )(wants, slices)


def pair_sums(core, factors, mine, other, screened, first, pairs, carried, last):
    _, slots, _, rows, cols = mine.shape
    times, _, blk, _ = screened.shape
    norb = factors.shape[-1]
    strip = 256

    def kernel(core_ref, *refs):
        if carried is None:
            fac, mine_ref, other_ref, tile, out, left, right, left_t, inner, acc = refs
        else:
            fac, mine_ref, other_ref, tile, start, out, left, right, left_t, inner, acc = refs
        p = pl.program_id(0)
        t = pl.program_id(1)
        own = core_ref[0]

        @pl.when((p == 0) & (t == 0))
        def _():
            if carried is None:
                acc[...] = jnp.zeros(acc.shape, acc.dtype)
            else:
                acc[...] = start[...]

        @pl.when(t == 0)
        def _():
            for source, side in ((mine_ref, own), (other_ref, 1 - own)):
                for half in range(2):
                    at = pl.multiple_of((half * 2 + side) * cols, cols)
                    left[:, pl.ds(at, cols)] = source[half, :, 0].reshape(blk, cols)
                    right[:, pl.ds(at, cols)] = source[half, :, 1].reshape(blk, cols)
            left_t[...] = left[...].T

        scale = fac[0, pl.ds(t, 1), :]
        whole = right[...]
        for s in range(blk // strip):
            part = slice(s * strip, (s + 1) * strip)
            scaled = (left[part, :].astype(jnp.float32) * scale).astype(jnp.bfloat16)
            green = lax.dot_general(
                scaled, whole, (((1,), (1,)), ((), ())), preferred_element_type=jnp.float32
            )
            product = (green * tile[0, 0, part, :].astype(jnp.float32)).astype(jnp.bfloat16)
            inner[part, :] = jnp.dot(product, whole, preferred_element_type=jnp.float32).astype(
                jnp.bfloat16
            )
        acc[t] += jnp.dot(left_t[...], inner[...], preferred_element_type=jnp.float32)

        @pl.when(p == pairs - 1)
        def _():
            total = acc[t]
            if last:
                both = (total + total.T).astype(out.dtype)
                out[:, t] = both.reshape(out.shape[0], out.shape[2], norb)
            else:
                out[t] = total

    own_rows = norb // slots
    if last:
        out_shape = jax.ShapeDtypeStruct((slots, times, own_rows, norb), jnp.bfloat16)
    else:
        out_shape = jax.ShapeDtypeStruct((times, norb, norb), jnp.float32)
    ends = len(out_shape.shape)
    blocks = pl.BlockSpec((2, slots, 2, rows, cols), lambda p, t, c: (0, 0, p, 0, 0))
    in_specs = [
        pl.BlockSpec((1, times, norb), lambda p, t, c: (first + p, 0, 0)),
        blocks,
        blocks,
        pl.BlockSpec((1, 1, blk, blk), lambda p, t, c: (t, first + p, 0, 0)),
    ]
    operands = [core, factors, mine, other, screened]
    if carried is not None:
        in_specs.append(pl.BlockSpec(carried.shape, lambda p, t, c: (0, 0, 0)))
        operands.append(carried)
    return pl.pallas_call(
        kernel,
        grid_spec=pltpu.PrefetchScalarGridSpec(
            num_scalar_prefetch=1,
            grid=(pairs, times),
            in_specs=in_specs,
            out_specs=pl.BlockSpec(out_shape.shape, lambda p, t, c: (0,) * ends),
            scratch_shapes=[
                pltpu.VMEM((blk, norb), jnp.bfloat16),
                pltpu.VMEM((blk, norb), jnp.bfloat16),
                pltpu.VMEM((norb, blk), jnp.bfloat16),
                pltpu.VMEM((blk, norb), jnp.bfloat16),
                pltpu.VMEM((times, norb, norb), jnp.float32),
            ],
        ),
        out_shape=out_shape,
        compiler_params=pltpu.CompilerParams(
            vmem_limit_bytes=48 << 20, dimension_semantics=("arbitrary", "arbitrary")
        ),
    )(*operands)


def shards(orbitals, level_gap, screened, pair_blocks):
    owners = lax.axis_size(PAIR)
    cols = orbitals.shape[1]
    rows = orbitals.shape[0] // owners
    time_local, pair_local = screened.shape[:2]
    norb = level_gap.shape[0]

    asked = jnp.zeros((INDEX_ROWS, cols), jnp.bfloat16)
    asked = asked.at[0, : 2 * pair_local].set(pair_blocks.reshape(-1).astype(jnp.bfloat16))
    sent = jnp.concatenate(
        [
            orbitals.reshape(owners, rows, cols),
            jnp.broadcast_to(asked, (owners, INDEX_ROWS, cols)),
        ],
        axis=1,
    )
    slices = lax.all_to_all(sent, PAIR, 0, 0, tiled=True)
    wants = slices[:, rows, : 2 * pair_local].astype(jnp.int32)

    group = lax.axis_index(("zh", "core"))
    core = lax.axis_index("core").astype(jnp.int32).reshape(1)
    moments = (group * time_local + jnp.arange(time_local)).astype(jnp.float32)
    tau = 6.0 * (moments + 0.5) / (time_local * lax.axis_size(("zh", "core")))
    signs = jnp.where(jnp.arange(norb) < NOCC, 1.0, -1.0).astype(jnp.float32)
    weights = jnp.where(pair_blocks[:, 0] == pair_blocks[:, 1], 0.5, 1.0).astype(jnp.float32)
    factors = signs[None, :] * jnp.exp(-level_gap[None, :] * tau[:, None])
    factors = weights[:, None, None] * factors[None]

    total = None
    for first, pairs in CHUNKS:
        picked = picked_for(wants, slices, 2 * first, 2 * pairs)
        picked = picked.reshape(2 * owners, 2 * pairs, rows, cols)
        mine = lax.all_to_all(picked, SAME_CORE, 0, 0, tiled=True)
        other = lax.ppermute(mine, "core", [(0, 1), (1, 0)])
        shape = (2, owners, 2 * pairs, rows, cols)
        last = first + pairs == pair_local
        total = pair_sums(
            core, factors, mine.reshape(shape), other.reshape(shape), screened, first, pairs, total, last
        )
    shares = lax.all_to_all(total, PAIR, 0, 0, tiled=True)
    return jnp.sum(shares.astype(jnp.float32), axis=0)


def solution(mesh):
    fine = Mesh(mesh.devices.reshape(2, 2, 2, 4, 4), ("zh", "core", "zl", "y", "x"))
    tm = ("zh", "core")
    placed = (P(PAIR, tm), P(), P(tm, PAIR, None, None), P(PAIR, None))
    return jax.shard_map(
        shards, mesh=fine, in_specs=placed, out_specs=P(tm, PAIR, None), check_vma=False
    )
```

```python
import jax
import jax.numpy as jnp
from jax import lax
from jax.experimental import pallas as pl
from jax.experimental.pallas import tpu as pltpu
from jax.sharding import Mesh
from jax.sharding import PartitionSpec as P

NOCC = 128
PAIR = ("zl", "y", "x")
SAME_CORE = ("zh", "zl", "y", "x")
CHUNKS = ((0, 3), (3, 1))
INDEX_ROWS = 8


def in_hbm(array):
    return pltpu.with_memory_space_constraint(array, pltpu.HBM)


def picked_for(wants, slices, first, count):
    owners, rows, cols = slices.shape[0], slices.shape[1] - INDEX_ROWS, slices.shape[2]
    per_step = 4

    def kernel(wants_ref, slices_ref, out_ref, sent):
        def some(i, unused):
            for d in range(per_step):
                for k in range(count):
                    block = wants_ref[i * per_step + d, first + k]
                    piece = slices_ref.at[block, pl.ds(0, rows), :]
                    for half in range(2):
                        at = out_ref.at[half, i * per_step + d, k]
                        pltpu.make_async_copy(piece, at, sent).start()
            return unused

        lax.fori_loop(0, owners // per_step, some, 0)
        pltpu.make_async_copy(out_ref, out_ref, sent).wait()

    return pl.pallas_call(
        kernel,
        grid_spec=pltpu.PrefetchScalarGridSpec(
            num_scalar_prefetch=1,
            grid=(1,),
            in_specs=[pl.BlockSpec(memory_space=pltpu.VMEM)],
            out_specs=pl.BlockSpec(memory_space=pltpu.HBM),
            scratch_shapes=[pltpu.SemaphoreType.DMA(())],
        ),
        out_shape=pltpu.HBM((2, owners, count, rows, cols), slices.dtype),
        compiler_params=pltpu.CompilerParams(vmem_limit_bytes=16 << 20),
    )(wants, slices)


def pair_sums(core, factors, mine, other, screened, first, carried, last):
    _, slots, blocks, rows, cols = mine.shape
    pairs = blocks // 2
    times, _, blk, _ = screened.shape
    norb = factors.shape[-1]
    strip = 256

    def kernel(core_ref, fac, mine_ref, other_ref, tile, *refs):
        start = None
        if carried is not None:
            start, *refs = refs
        out, left, right, left_t, inner, acc, moved = refs
        p = pl.program_id(0)
        t = pl.program_id(1)
        own = core_ref[0]
        opens = (p == 0) & (t == 0)

        @pl.when(opens)
        def _():
            if start is None:
                acc[...] = jnp.zeros(acc.shape, acc.dtype)
            else:
                pltpu.make_async_copy(start, acc, moved.at[0]).start()

        @pl.when(t == 0)
        def _():
            for source, side in ((mine_ref, own), (other_ref, 1 - own)):
                for half in range(2):
                    at = pl.multiple_of((half * 2 + side) * cols, cols)
                    left[:, pl.ds(at, cols)] = source[half, :, 0].reshape(blk, cols)
                    right[:, pl.ds(at, cols)] = source[half, :, 1].reshape(blk, cols)
            left_t[...] = left[...].T

        scale = fac[0, pl.ds(t, 1), :]
        whole = right[...]
        for s in range(blk // strip):
            part = slice(s * strip, (s + 1) * strip)
            scaled = (left[part, :].astype(jnp.float32) * scale).astype(jnp.bfloat16)
            green = lax.dot_general(
                scaled, whole, (((1,), (1,)), ((), ())), preferred_element_type=jnp.float32
            )
            product = (green * tile[0, 0, part, :].astype(jnp.float32)).astype(jnp.bfloat16)
            inner[part, :] = jnp.dot(product, whole, preferred_element_type=jnp.float32).astype(
                jnp.bfloat16
            )

        if start is not None:

            @pl.when(opens)
            def _():
                pltpu.make_async_copy(start, acc, moved.at[0]).wait()

        acc[t] += jnp.dot(left_t[...], inner[...], preferred_element_type=jnp.float32)

        if last:

            @pl.when(p == pairs - 1)
            def _():
                total = acc[t]
                both = (total + total.T).astype(out.dtype)
                out[:, t] = both.reshape(out.shape[0], out.shape[2], norb)

        else:

            @pl.when(p == pairs - 1)
            def _():
                pltpu.make_async_copy(acc.at[t], out.at[t], moved.at[t]).start()

            @pl.when((p == pairs - 1) & (t == times - 1))
            def _():
                for k in range(times):
                    pltpu.make_async_copy(acc.at[k], out.at[k], moved.at[k]).wait()

    sums = (times, norb, norb)
    if last:
        out_shape = jax.ShapeDtypeStruct((slots, times, norb // slots, norb), jnp.bfloat16)
        out_spec = pl.BlockSpec(out_shape.shape, lambda p, t, c: (0, 0, 0, 0))
    else:
        out_shape = pltpu.HBM(sums, jnp.float32)
        out_spec = pl.BlockSpec(memory_space=pltpu.HBM)
    operands = [core, factors, mine, other, in_hbm(screened)]
    brought = pl.BlockSpec((2, slots, 2, rows, cols), lambda p, t, c: (0, 0, p, 0, 0))
    in_specs = [
        pl.BlockSpec((1, times, norb), lambda p, t, c: (first + p, 0, 0)),
        brought,
        brought,
        pl.BlockSpec((1, 1, blk, blk), lambda p, t, c: (t, first + p, 0, 0)),
    ]
    if carried is not None:
        operands.append(in_hbm(carried))
        in_specs.append(pl.BlockSpec(memory_space=pltpu.HBM))
    return pl.pallas_call(
        kernel,
        grid_spec=pltpu.PrefetchScalarGridSpec(
            num_scalar_prefetch=1,
            grid=(pairs, times),
            in_specs=in_specs,
            out_specs=out_spec,
            scratch_shapes=[
                pltpu.VMEM((blk, norb), jnp.bfloat16),
                pltpu.VMEM((blk, norb), jnp.bfloat16),
                pltpu.VMEM((norb, blk), jnp.bfloat16),
                pltpu.VMEM((blk, norb), jnp.bfloat16),
                pltpu.VMEM(sums, jnp.float32),
                pltpu.SemaphoreType.DMA((times,)),
            ],
        ),
        out_shape=out_shape,
        compiler_params=pltpu.CompilerParams(
            vmem_limit_bytes=32 << 20, dimension_semantics=("arbitrary", "arbitrary")
        ),
    )(*operands)


def shards(orbitals, level_gap, screened, pair_blocks):
    owners = lax.axis_size(PAIR)
    cols = orbitals.shape[1]
    rows = orbitals.shape[0] // owners
    time_local, pair_local = screened.shape[:2]
    norb = level_gap.shape[0]

    asked = jnp.zeros((INDEX_ROWS, cols), jnp.bfloat16)
    asked = asked.at[0, : 2 * pair_local].set(pair_blocks.reshape(-1).astype(jnp.bfloat16))
    sent = jnp.concatenate(
        [
            orbitals.reshape(owners, rows, cols),
            jnp.broadcast_to(asked, (owners, INDEX_ROWS, cols)),
        ],
        axis=1,
    )
    slices = lax.all_to_all(sent, PAIR, 0, 0, tiled=True)
    wants = slices[:, rows, : 2 * pair_local].astype(jnp.int32)

    group = lax.axis_index(("zh", "core"))
    core = lax.axis_index("core").astype(jnp.int32).reshape(1)
    moments = (group * time_local + jnp.arange(time_local)).astype(jnp.float32)
    tau = 6.0 * (moments + 0.5) / (time_local * lax.axis_size(("zh", "core")))
    signs = jnp.where(jnp.arange(norb) < NOCC, 1.0, -1.0).astype(jnp.float32)
    weights = jnp.where(pair_blocks[:, 0] == pair_blocks[:, 1], 0.5, 1.0).astype(jnp.float32)
    factors = signs[None, :] * jnp.exp(-level_gap[None, :] * tau[:, None])
    factors = weights[:, None, None] * factors[None]

    total = None
    for first, pairs in CHUNKS:
        picked = picked_for(wants, slices, 2 * first, 2 * pairs)
        picked = picked.reshape(2 * owners, 2 * pairs, rows, cols)
        mine = lax.all_to_all(picked, SAME_CORE, 0, 0, tiled=True)
        other = lax.ppermute(mine, "core", [(0, 1), (1, 0)])
        shape = (2, owners, 2 * pairs, rows, cols)
        last = first + pairs == pair_local
        total = pair_sums(
            core, factors, mine.reshape(shape), other.reshape(shape), screened, first, total, last
        )
    shares = lax.all_to_all(total, PAIR, 0, 0, tiled=True)
    return jnp.sum(shares.astype(jnp.float32), axis=0)


def solution(mesh):
    fine = Mesh(mesh.devices.reshape(2, 2, 2, 4, 4), ("zh", "core", "zl", "y", "x"))
    tm = ("zh", "core")
    placed = (P(PAIR, tm), P(), P(tm, PAIR, None, None), P(PAIR, None))
    return jax.shard_map(
        shards, mesh=fine, in_specs=placed, out_specs=P(tm, PAIR, None), check_vma=False
    )
```

```python
import jax
import jax.numpy as jnp
from jax import lax
from jax.experimental import pallas as pl
from jax.experimental.pallas import tpu as pltpu
from jax.sharding import Mesh
from jax.sharding import PartitionSpec as P

NOCC = 128
PAIR = ("zl", "y", "x")
SAME_CORE = ("zh", "zl", "y", "x")
INDEX_ROWS = 8
FIRST = ((0, 1, 2), (3, 1, 2))


def in_hbm(array):
    return pltpu.with_memory_space_constraint(array, pltpu.HBM)


def picked_for(wants, slices):
    owners, rows, cols = slices.shape[0], slices.shape[1] - INDEX_ROWS, slices.shape[2]
    count = 2 * len(FIRST[0])
    per_step = 4

    def kernel(wants_ref, slices_ref, out_ref, sent):
        def some(i, unused):
            for d in range(per_step):
                for half in range(2):
                    for k in range(count):
                        block = wants_ref[i * per_step + d, 2 * FIRST[half][k // 2] + k % 2]
                        piece = slices_ref.at[block, pl.ds(0, rows), :]
                        at = out_ref.at[half, i * per_step + d, k]
                        pltpu.make_async_copy(piece, at, sent).start()
            return unused

        lax.fori_loop(0, owners // per_step, some, 0)
        pltpu.make_async_copy(out_ref, out_ref, sent).wait()

    return pl.pallas_call(
        kernel,
        grid_spec=pltpu.PrefetchScalarGridSpec(
            num_scalar_prefetch=1,
            grid=(1,),
            in_specs=[pl.BlockSpec(memory_space=pltpu.VMEM)],
            out_specs=pl.BlockSpec(memory_space=pltpu.HBM),
            scratch_shapes=[pltpu.SemaphoreType.DMA(())],
        ),
        out_shape=pltpu.HBM((2, owners, count, rows, cols), slices.dtype),
        compiler_params=pltpu.CompilerParams(vmem_limit_bytes=16 << 20),
    )(wants, slices)


def pair_sums(where, factors, mine, other, screened, carried):
    _, slots, blocks, rows, cols = mine.shape
    pairs = blocks // 2
    times, _, blk, _ = screened.shape
    norb = factors.shape[-1]
    strip = 256
    last = carried is not None

    def kernel(where_ref, fac, mine_ref, other_ref, screened_ref, *refs):
        start = None
        if last:
            start, *refs = refs
        out, left, right, inner, tiles, acc, got, seen, moved = refs
        p = pl.program_id(0)
        slot = lax.rem(p, 2)
        own = where_ref[0]

        def at_first(do):
            do() if pairs == 1 else pl.when(p == 0)(do)

        def at_last(do):
            do() if pairs == 1 else pl.when(p == pairs - 1)(do)

        def bring(q, to):
            for source, side in ((mine_ref, own), (other_ref, 1 - own)):
                for half in range(2):
                    at = pl.multiple_of((half * 2 + side) * cols, cols)
                    for b, target in enumerate((left, right)):
                        pltpu.make_async_copy(
                            source.at[half, :, 2 * q + b],
                            target.at[to, :, :, pl.ds(at, cols)],
                            got.at[b, to],
                        ).start()
            for t in range(times):
                tile(q, t, to).start()

        def tile(q, t, to):
            return pltpu.make_async_copy(
                screened_ref.at[t, where_ref[1 + q]], tiles.at[to, t], seen.at[to, t]
            )

        @at_first
        def _():
            bring(0, 0)
            if last:
                pltpu.make_async_copy(start, acc, moved.at[0]).start()
            else:
                acc[...] = jnp.zeros(acc.shape, acc.dtype)

        if pairs > 1:

            @pl.when(p + 1 < pairs)
            def _():
                bring(p + 1, 1 - slot)

        for b, target in enumerate((left, right)):
            pltpu.make_async_copy(target.at[slot], target.at[slot], got.at[b, slot]).wait()
        left_side = left[slot].reshape(blk, norb)
        right_side = right[slot].reshape(blk, norb)
        for t in range(times):
            tile(p, t, slot).wait()
            scale = fac[0, t : t + 1, :]
            for s in range(blk // strip):
                part = slice(s * strip, (s + 1) * strip)
                scaled = (left_side[part, :].astype(jnp.float32) * scale).astype(jnp.bfloat16)
                green = lax.dot_general(
                    scaled, right_side, (((1,), (1,)), ((), ())), preferred_element_type=jnp.float32
                )
                product = (green * tiles[slot, t, part, :].astype(jnp.float32)).astype(jnp.bfloat16)
                inner[t, part, :] = jnp.dot(
                    product, right_side, preferred_element_type=jnp.float32
                ).astype(jnp.bfloat16)
            if last and t == 0:

                @at_first
                def _():
                    pltpu.make_async_copy(start, acc, moved.at[0]).wait()

            acc[t] += lax.dot_general(
                left_side, inner[t], (((0,), (0,)), ((), ())), preferred_element_type=jnp.float32
            )

        @at_last
        def _():
            if last:
                for t in range(times):
                    total = acc[t]
                    both = (total + total.T).astype(out.dtype)
                    out[:, t] = both.reshape(out.shape[0], out.shape[2], norb)
            else:
                copies = [
                    pltpu.make_async_copy(acc.at[t], out.at[t], moved.at[t]) for t in range(times)
                ]
                for copy in copies:
                    copy.start()
                for copy in copies:
                    copy.wait()

    sums = (times, norb, norb)
    outside = pl.BlockSpec(memory_space=pltpu.HBM)
    anywhere = pl.BlockSpec(memory_space=pl.ANY)
    if last:
        out_shape = jax.ShapeDtypeStruct((slots, times, norb // slots, norb), jnp.bfloat16)
        out_spec = pl.BlockSpec(out_shape.shape, lambda p, c: (0, 0, 0, 0))
    else:
        out_shape = pltpu.HBM(sums, jnp.float32)
        out_spec = outside
    operands = [where, factors, mine, other, in_hbm(screened)]
    if last:
        operands.append(in_hbm(carried))
    return pl.pallas_call(
        kernel,
        grid_spec=pltpu.PrefetchScalarGridSpec(
            num_scalar_prefetch=1,
            grid=(pairs,),
            in_specs=[pl.BlockSpec((1, times, norb), lambda p, c: (c[1 + p], 0, 0))]
            + [anywhere] * 2
            + [outside] * (len(operands) - 4),
            out_specs=out_spec,
            scratch_shapes=[
                pltpu.VMEM((2, slots, rows, norb), jnp.bfloat16),
                pltpu.VMEM((2, slots, rows, norb), jnp.bfloat16),
                pltpu.VMEM((times, blk, norb), jnp.bfloat16),
                pltpu.VMEM((2, times, blk, blk), jnp.bfloat16),
                pltpu.VMEM(sums, jnp.float32),
                pltpu.SemaphoreType.DMA((2, 2)),
                pltpu.SemaphoreType.DMA((2, times)),
                pltpu.SemaphoreType.DMA((times,)),
            ],
        ),
        out_shape=out_shape,
        compiler_params=pltpu.CompilerParams(
            vmem_limit_bytes=40 << 20, dimension_semantics=("arbitrary",)
        ),
    )(*operands)


def shards(orbitals, level_gap, screened, pair_blocks):
    owners = lax.axis_size(PAIR)
    cols = orbitals.shape[1]
    rows = orbitals.shape[0] // owners
    time_local, pair_local = screened.shape[:2]
    norb = level_gap.shape[0]

    asked = jnp.zeros((INDEX_ROWS, cols), jnp.bfloat16)
    asked = asked.at[0, : 2 * pair_local].set(pair_blocks.reshape(-1).astype(jnp.bfloat16))
    sent = jnp.concatenate(
        [
            orbitals.reshape(owners, rows, cols),
            jnp.broadcast_to(asked, (owners, INDEX_ROWS, cols)),
        ],
        axis=1,
    )
    slices = lax.all_to_all(sent, PAIR, 0, 0, tiled=True)
    wants = slices[:, rows, : 2 * pair_local].astype(jnp.int32)

    half = lax.axis_index("zh")
    core = lax.axis_index("core")
    first = jnp.where(half == 0, FIRST[0][0], FIRST[1][0])
    final = jnp.where(half == 0, FIRST[1][0], FIRST[0][0])
    opening = jnp.stack([core, first, FIRST[0][1], FIRST[0][2]]).astype(jnp.int32)
    closing = jnp.stack([core, final]).astype(jnp.int32)
    swap = [(0, 1), (1, 0)]
    picked = picked_for(wants, slices).reshape(2 * owners, -1, rows, cols)
    mine = lax.all_to_all(picked, SAME_CORE, 0, 0, tiled=True)
    moments = ((half * 2 + core) * time_local + jnp.arange(time_local)).astype(jnp.float32)
    tau = 6.0 * (moments + 0.5) / (time_local * lax.axis_size(("zh", "core")))
    signs = jnp.where(jnp.arange(norb) < NOCC, 1.0, -1.0).astype(jnp.float32)
    weights = jnp.where(pair_blocks[:, 0] == pair_blocks[:, 1], 0.5, 1.0).astype(jnp.float32)
    factors = signs[None, :] * jnp.exp(-level_gap[None, :] * tau[:, None])
    factors = weights[:, None, None] * factors[None]
    other = lax.ppermute(mine, "core", swap)
    traded = lax.ppermute(mine[:, :2], "zh", swap)
    shape = (2, owners, -1, rows, cols)
    total = pair_sums(opening, factors, mine.reshape(shape), other.reshape(shape), screened, None)
    twin = lax.ppermute(traded, "core", swap)
    total = pair_sums(closing, factors, traded.reshape(shape), twin.reshape(shape), screened, total)
    shares = lax.all_to_all(total, PAIR, 0, 0, tiled=True)
    return jnp.sum(shares.astype(jnp.float32), axis=0)


def solution(mesh):
    fine = Mesh(mesh.devices.reshape(2, 2, 2, 4, 4), ("zh", "core", "zl", "y", "x"))
    tm = ("zh", "core")
    placed = (P(PAIR, tm), P(), P(tm, PAIR, None, None), P(PAIR, None))
    return jax.shard_map(
        shards, mesh=fine, in_specs=placed, out_specs=P(tm, PAIR, None), check_vma=False
    )
```

```python
import jax
import jax.numpy as jnp
from jax import lax
from jax.experimental import pallas as pl
from jax.experimental.pallas import tpu as pltpu
from jax.sharding import Mesh
from jax.sharding import PartitionSpec as P

NOCC = 128
PAIR = ("zl", "y", "x")
SAME_CORE = ("zh", "zl", "y", "x")
INDEX_ROWS = 8
FIRST = ((0, 1, 2), (3, 1, 2))


def in_hbm(array):
    return pltpu.with_memory_space_constraint(array, pltpu.HBM)


def picked_for(wants, slices):
    owners, rows, cols = slices.shape[0], slices.shape[1] - INDEX_ROWS, slices.shape[2]
    count = 2 * len(FIRST[0])
    per_step = 4

    def kernel(wants_ref, slices_ref, out_ref, sent):
        def some(i, unused):
            for d in range(per_step):
                for half in range(2):
                    for k in range(count):
                        block = wants_ref[i * per_step + d, 2 * FIRST[half][k // 2] + k % 2]
                        piece = slices_ref.at[block, pl.ds(0, rows), :]
                        at = out_ref.at[half, i * per_step + d, k]
                        pltpu.make_async_copy(piece, at, sent).start()
            return unused

        lax.fori_loop(0, owners // per_step, some, 0)
        pltpu.make_async_copy(out_ref, out_ref, sent).wait()

    return pl.pallas_call(
        kernel,
        grid_spec=pltpu.PrefetchScalarGridSpec(
            num_scalar_prefetch=1,
            grid=(1,),
            in_specs=[pl.BlockSpec(memory_space=pltpu.VMEM)],
            out_specs=pl.BlockSpec(memory_space=pltpu.HBM),
            scratch_shapes=[pltpu.SemaphoreType.DMA(())],
        ),
        out_shape=pltpu.HBM((2, owners, count, rows, cols), slices.dtype),
        compiler_params=pltpu.CompilerParams(vmem_limit_bytes=16 << 20),
    )(wants, slices)


def pair_sums(where, factors, mine, other, screened, carried):
    _, slots, blocks, rows, cols = mine.shape
    pairs = blocks // 2
    times, _, blk, _ = screened.shape
    norb = factors.shape[-1]
    strip = 256
    last = carried is not None

    def kernel(where_ref, fac, mine_ref, other_ref, *refs):
        if last:
            start, tiles, out, left, right, inner, got = refs
        else:
            screened_ref, out, ahead, left, right, inner, tiles, got, seen, moved = refs
        p = pl.program_id(0)
        slot = 0 if last else lax.rem(p, 2)
        own = where_ref[0]

        def bring(q, to):
            for source, side in ((mine_ref, own), (other_ref, 1 - own)):
                for half in range(2):
                    at = pl.multiple_of((half * 2 + side) * cols, cols)
                    for b, target in enumerate((left, right)):
                        pltpu.make_async_copy(
                            source.at[half, :, 2 * q + b],
                            target.at[to, :, :, pl.ds(at, cols)],
                            got.at[b, to],
                        ).start()
            if not last:
                for t in range(times):
                    tile(q, t, to).start()

        def tile(q, t, to):
            return pltpu.make_async_copy(
                screened_ref.at[t, where_ref[1 + q]], tiles.at[to, t], seen.at[to, t]
            )

        def later(t):
            return pltpu.make_async_copy(
                screened_ref.at[t, where_ref[1 + pairs]], ahead.at[t], moved.at[t]
            )

        if last:
            bring(0, 0)
        else:

            @pl.when(p == 0)
            def _():
                bring(0, 0)
                for t in range(times):
                    later(t).start()
                out[...] = jnp.zeros(out.shape, out.dtype)

            @pl.when(p + 1 < pairs)
            def _():
                bring(p + 1, 1 - slot)

        for b, target in enumerate((left, right)):
            pltpu.make_async_copy(target.at[slot], target.at[slot], got.at[b, slot]).wait()
        left_side = left[slot].reshape(blk, norb)
        right_side = right[slot].reshape(blk, norb)
        for t in range(times):
            if not last:
                tile(p, t, slot).wait()
            scale = fac[0, t : t + 1, :]
            for s in range(blk // strip):
                part = slice(s * strip, (s + 1) * strip)
                scaled = (left_side[part, :].astype(jnp.float32) * scale).astype(jnp.bfloat16)
                green = lax.dot_general(
                    scaled, right_side, (((1,), (1,)), ((), ())), preferred_element_type=jnp.float32
                )
                held = tiles[t, part, :] if last else tiles[slot, t, part, :]
                product = (green * held.astype(jnp.float32)).astype(jnp.bfloat16)
                inner[t, part, :] = jnp.dot(
                    product, right_side, preferred_element_type=jnp.float32
                ).astype(jnp.bfloat16)
            added = lax.dot_general(
                left_side, inner[t], (((0,), (0,)), ((), ())), preferred_element_type=jnp.float32
            )
            if last:
                total = start[t] + added
                both = (total + total.T).astype(out.dtype)
                out[:, t] = both.reshape(out.shape[0], out.shape[2], norb)
            else:
                out[t] += added

        if not last:

            @pl.when(p == pairs - 1)
            def _():
                for t in range(times):
                    later(t).wait()

    sums = (times, norb, norb)
    here = pl.BlockSpec(memory_space=pltpu.VMEM)
    anywhere = pl.BlockSpec(memory_space=pl.ANY)
    buffers = 1 if last else 2
    scratch = [
        pltpu.VMEM((buffers, slots, rows, norb), jnp.bfloat16),
        pltpu.VMEM((buffers, slots, rows, norb), jnp.bfloat16),
        pltpu.VMEM((times, blk, norb), jnp.bfloat16),
    ]
    if last:
        operands, specs = list(carried), [here, here]
        scratch += [pltpu.SemaphoreType.DMA((2, buffers))]
        out_shape = jax.ShapeDtypeStruct((slots, times, norb // slots, norb), jnp.bfloat16)
        out_specs = here
    else:
        operands, specs = [in_hbm(screened)], [pl.BlockSpec(memory_space=pltpu.HBM)]
        scratch += [
            pltpu.VMEM((buffers, times, blk, blk), jnp.bfloat16),
            pltpu.SemaphoreType.DMA((2, buffers)),
            pltpu.SemaphoreType.DMA((buffers, times)),
            pltpu.SemaphoreType.DMA((times,)),
        ]
        out_shape = (
            jax.ShapeDtypeStruct(sums, jnp.float32),
            jax.ShapeDtypeStruct((times, blk, blk), jnp.bfloat16),
        )
        out_specs = (here, here)
    return pl.pallas_call(
        kernel,
        grid_spec=pltpu.PrefetchScalarGridSpec(
            num_scalar_prefetch=1,
            grid=(pairs,),
            in_specs=[
                pl.BlockSpec((1, times, norb), lambda p, c: (c[1 + p], 0, 0)),
                anywhere,
                anywhere,
            ]
            + specs,
            out_specs=out_specs,
            scratch_shapes=scratch,
        ),
        out_shape=out_shape,
        compiler_params=pltpu.CompilerParams(
            vmem_limit_bytes=40 << 20, dimension_semantics=("arbitrary",)
        ),
    )(where, factors, mine, other, *operands)


def shards(orbitals, level_gap, screened, pair_blocks):
    owners = lax.axis_size(PAIR)
    cols = orbitals.shape[1]
    rows = orbitals.shape[0] // owners
    time_local, pair_local = screened.shape[:2]
    norb = level_gap.shape[0]

    asked = jnp.zeros((INDEX_ROWS, cols), jnp.bfloat16)
    asked = asked.at[0, : 2 * pair_local].set(pair_blocks.reshape(-1).astype(jnp.bfloat16))
    sent = jnp.concatenate(
        [
            orbitals.reshape(owners, rows, cols),
            jnp.broadcast_to(asked, (owners, INDEX_ROWS, cols)),
        ],
        axis=1,
    )
    slices = lax.all_to_all(sent, PAIR, 0, 0, tiled=True)
    wants = slices[:, rows, : 2 * pair_local].astype(jnp.int32)

    half = lax.axis_index("zh")
    core = lax.axis_index("core")
    first = jnp.where(half == 0, FIRST[0][0], FIRST[1][0])
    final = jnp.where(half == 0, FIRST[1][0], FIRST[0][0])
    opening = jnp.stack([core, first, FIRST[0][1], FIRST[0][2], final]).astype(jnp.int32)
    closing = jnp.stack([core, final]).astype(jnp.int32)
    swap = [(0, 1), (1, 0)]
    picked = picked_for(wants, slices).reshape(2 * owners, -1, rows, cols)
    mine = lax.all_to_all(picked, SAME_CORE, 0, 0, tiled=True)
    moments = ((half * 2 + core) * time_local + jnp.arange(time_local)).astype(jnp.float32)
    tau = 6.0 * (moments + 0.5) / (time_local * lax.axis_size(("zh", "core")))
    signs = jnp.where(jnp.arange(norb) < NOCC, 1.0, -1.0).astype(jnp.float32)
    weights = jnp.where(pair_blocks[:, 0] == pair_blocks[:, 1], 0.5, 1.0).astype(jnp.float32)
    factors = signs[None, :] * jnp.exp(-level_gap[None, :] * tau[:, None])
    factors = weights[:, None, None] * factors[None]
    other = lax.ppermute(mine, "core", swap)
    traded = lax.ppermute(mine[:, :2], "zh", swap)
    shape = (2, owners, -1, rows, cols)
    kept = pair_sums(opening, factors, mine.reshape(shape), other.reshape(shape), screened, None)
    twin = lax.ppermute(traded, "core", swap)
    total = pair_sums(closing, factors, traded.reshape(shape), twin.reshape(shape), screened, kept)
    shares = lax.all_to_all(total, PAIR, 0, 0, tiled=True)
    return jnp.sum(shares.astype(jnp.float32), axis=0)


def solution(mesh):
    fine = Mesh(mesh.devices.reshape(2, 2, 2, 4, 4), ("zh", "core", "zl", "y", "x"))
    tm = ("zh", "core")
    placed = (P(PAIR, tm), P(), P(tm, PAIR, None, None), P(PAIR, None))
    return jax.shard_map(
        shards, mesh=fine, in_specs=placed, out_specs=P(tm, PAIR, None), check_vma=False
    )
```

```python
import jax
import jax.numpy as jnp
from jax import lax
from jax.experimental import pallas as pl
from jax.experimental.pallas import tpu as pltpu
from jax.sharding import Mesh
from jax.sharding import PartitionSpec as P

NOCC = 128
PAIR = ("zl", "y", "x")
SAME_CORE = ("zh", "zl", "y", "x")
INDEX_ROWS = 8
FIRST = ((0, 1, 2), (3, 1, 2))


def in_hbm(array):
    return pltpu.with_memory_space_constraint(array, pltpu.HBM)


def picked_for(wants, slices):
    owners, rows, cols = slices.shape[0], slices.shape[1] - INDEX_ROWS, slices.shape[2]
    count = 2 * len(FIRST[0])
    per_step = 4

    def kernel(wants_ref, slices_ref, out_ref, sent):
        def some(i, unused):
            for d in range(per_step):
                for half in range(2):
                    for k in range(count):
                        block = wants_ref[i * per_step + d, 2 * FIRST[half][k // 2] + k % 2]
                        piece = slices_ref.at[block, pl.ds(0, rows), :]
                        at = out_ref.at[half, i * per_step + d, k]
                        pltpu.make_async_copy(piece, at, sent).start()
            return unused

        lax.fori_loop(0, owners // per_step, some, 0)
        pltpu.make_async_copy(out_ref, out_ref, sent).wait()

    return pl.pallas_call(
        kernel,
        grid_spec=pltpu.PrefetchScalarGridSpec(
            num_scalar_prefetch=1,
            grid=(1,),
            in_specs=[pl.BlockSpec(memory_space=pltpu.VMEM)],
            out_specs=pl.BlockSpec(memory_space=pltpu.HBM),
            scratch_shapes=[pltpu.SemaphoreType.DMA(())],
        ),
        out_shape=pltpu.HBM((2, owners, count, rows, cols), slices.dtype),
        compiler_params=pltpu.CompilerParams(vmem_limit_bytes=16 << 20),
    )(wants, slices)


def pair_sums(where, factors, mine, other, screened, carried):
    _, slots, blocks, rows, cols = mine[0].shape
    parts = len(mine)
    pairs = blocks * parts // 2
    times, _, blk, _ = screened.shape
    norb = factors.shape[-1]
    strip = 256
    last = carried is not None

    def kernel(where_ref, fac, *refs):
        mine_refs, other_refs, refs = refs[:parts], refs[parts : 2 * parts], refs[2 * parts :]
        if last:
            start, tiles, out, left, right, inner, got = refs
        else:
            screened_ref, out, ahead, left, right, inner, tiles, got, seen, moved = refs
        p = pl.program_id(0)
        slot = 0 if last else lax.rem(p, 2)
        own = where_ref[0]

        def bring(q, to):
            for sources, side in ((mine_refs, own), (other_refs, 1 - own)):
                for half in range(2):
                    at = pl.multiple_of((half * 2 + side) * cols, cols)
                    for b, target in enumerate((left, right)):
                        pltpu.make_async_copy(
                            sources[b % parts].at[half, :, (2 * q + b) // parts],
                            target.at[to, :, :, pl.ds(at, cols)],
                            got.at[b, to],
                        ).start()
            if not last:
                for t in range(times):
                    tile(q, t, to).start()

        def tile(q, t, to):
            return pltpu.make_async_copy(
                screened_ref.at[t, where_ref[1 + q]], tiles.at[to, t], seen.at[to, t]
            )

        def later(t):
            return pltpu.make_async_copy(
                screened_ref.at[t, where_ref[1 + pairs]], ahead.at[t], moved.at[t]
            )

        if last:
            bring(0, 0)
        else:

            @pl.when(p == 0)
            def _():
                bring(0, 0)
                for t in range(times):
                    later(t).start()
                out[...] = jnp.zeros(out.shape, out.dtype)

            @pl.when(p + 1 < pairs)
            def _():
                bring(p + 1, 1 - slot)

        for b, target in enumerate((left, right)):
            pltpu.make_async_copy(target.at[slot], target.at[slot], got.at[b, slot]).wait()
        left_side = left[slot].reshape(blk, norb)
        right_side = right[slot].reshape(blk, norb)
        for t in range(times):
            if not last:
                tile(p, t, slot).wait()
            scale = fac[0, t : t + 1, :]
            for s in range(blk // strip):
                part = slice(s * strip, (s + 1) * strip)
                scaled = (left_side[part, :].astype(jnp.float32) * scale).astype(jnp.bfloat16)
                green = lax.dot_general(
                    scaled, right_side, (((1,), (1,)), ((), ())), preferred_element_type=jnp.float32
                )
                held = tiles[t, part, :] if last else tiles[slot, t, part, :]
                product = (green * held.astype(jnp.float32)).astype(jnp.bfloat16)
                inner[t, part, :] = jnp.dot(
                    product, right_side, preferred_element_type=jnp.float32
                ).astype(jnp.bfloat16)
            added = lax.dot_general(
                left_side, inner[t], (((0,), (0,)), ((), ())), preferred_element_type=jnp.float32
            )
            if last:
                total = start[t] + added
                both = (total + total.T).astype(out.dtype)
                out[:, t] = both.reshape(out.shape[0], out.shape[2], norb)
            else:
                out[t] += added

        if not last:

            @pl.when(p == pairs - 1)
            def _():
                for t in range(times):
                    later(t).wait()

    sums = (times, norb, norb)
    here = pl.BlockSpec(memory_space=pltpu.VMEM)
    anywhere = pl.BlockSpec(memory_space=pl.ANY)
    buffers = 1 if last else 2
    scratch = [
        pltpu.VMEM((buffers, slots, rows, norb), jnp.bfloat16),
        pltpu.VMEM((buffers, slots, rows, norb), jnp.bfloat16),
        pltpu.VMEM((times, blk, norb), jnp.bfloat16),
    ]
    if last:
        operands, specs = list(carried), [here, here]
        scratch += [pltpu.SemaphoreType.DMA((2, buffers))]
        out_shape = jax.ShapeDtypeStruct((slots, times, norb // slots, norb), jnp.bfloat16)
        out_specs = here
    else:
        operands, specs = [in_hbm(screened)], [pl.BlockSpec(memory_space=pltpu.HBM)]
        scratch += [
            pltpu.VMEM((buffers, times, blk, blk), jnp.bfloat16),
            pltpu.SemaphoreType.DMA((2, buffers)),
            pltpu.SemaphoreType.DMA((buffers, times)),
            pltpu.SemaphoreType.DMA((times,)),
        ]
        out_shape = (
            jax.ShapeDtypeStruct(sums, jnp.float32),
            jax.ShapeDtypeStruct((times, blk, blk), jnp.bfloat16),
        )
        out_specs = (here, here)
    return pl.pallas_call(
        kernel,
        grid_spec=pltpu.PrefetchScalarGridSpec(
            num_scalar_prefetch=1,
            grid=(pairs,),
            in_specs=[
                pl.BlockSpec((1, times, norb), lambda p, c: (c[1 + p], 0, 0)),
            ]
            + [anywhere] * (2 * parts)
            + specs,
            out_specs=out_specs,
            scratch_shapes=scratch,
        ),
        out_shape=out_shape,
        compiler_params=pltpu.CompilerParams(
            vmem_limit_bytes=40 << 20, dimension_semantics=("arbitrary",)
        ),
    )(where, factors, *mine, *other, *operands)


def shards(orbitals, level_gap, screened, pair_blocks):
    owners = lax.axis_size(PAIR)
    cols = orbitals.shape[1]
    rows = orbitals.shape[0] // owners
    time_local, pair_local = screened.shape[:2]
    norb = level_gap.shape[0]

    asked = jnp.zeros((INDEX_ROWS, cols), jnp.bfloat16)
    asked = asked.at[0, : 2 * pair_local].set(pair_blocks.reshape(-1).astype(jnp.bfloat16))
    sent = jnp.concatenate(
        [
            orbitals.reshape(owners, rows, cols),
            jnp.broadcast_to(asked, (owners, INDEX_ROWS, cols)),
        ],
        axis=1,
    )
    slices = lax.all_to_all(sent, PAIR, 0, 0, tiled=True)
    wants = slices[:, rows, : 2 * pair_local].astype(jnp.int32)

    half = lax.axis_index("zh")
    core = lax.axis_index("core")
    first = jnp.where(half == 0, FIRST[0][0], FIRST[1][0])
    final = jnp.where(half == 0, FIRST[1][0], FIRST[0][0])
    opening = jnp.stack([core, first, FIRST[0][1], FIRST[0][2], final]).astype(jnp.int32)
    closing = jnp.stack([core, final]).astype(jnp.int32)
    swap = [(0, 1), (1, 0)]
    picked = picked_for(wants, slices).reshape(2 * owners, -1, rows, cols)
    mine = lax.all_to_all(picked, SAME_CORE, 0, 0, tiled=True)
    moments = ((half * 2 + core) * time_local + jnp.arange(time_local)).astype(jnp.float32)
    tau = 6.0 * (moments + 0.5) / (time_local * lax.axis_size(("zh", "core")))
    signs = jnp.where(jnp.arange(norb) < NOCC, 1.0, -1.0).astype(jnp.float32)
    weights = jnp.where(pair_blocks[:, 0] == pair_blocks[:, 1], 0.5, 1.0).astype(jnp.float32)
    factors = signs[None, :] * jnp.exp(-level_gap[None, :] * tau[:, None])
    factors = weights[:, None, None] * factors[None]
    other = lax.ppermute(mine, "core", swap)
    traded, twins = [], []
    for b in range(2):
        traded.append(lax.ppermute(mine[:, b : b + 1], "zh", swap))
    shape = (2, owners, -1, rows, cols)
    kept = pair_sums(
        opening, factors, [mine.reshape(shape)], [other.reshape(shape)], screened, None
    )
    for b in range(2):
        twins.append(lax.ppermute(traded[b], "core", swap))
    traded = [part.reshape(shape) for part in traded]
    twins = [part.reshape(shape) for part in twins]
    total = pair_sums(closing, factors, traded, twins, screened, kept)
    shares = lax.all_to_all(total, PAIR, 0, 0, tiled=True)
    return jnp.sum(shares.astype(jnp.float32), axis=0)


def solution(mesh):
    fine = Mesh(mesh.devices.reshape(2, 2, 2, 4, 4), ("zh", "core", "zl", "y", "x"))
    tm = ("zh", "core")
    placed = (P(PAIR, tm), P(), P(tm, PAIR, None, None), P(PAIR, None))
    return jax.shard_map(
        shards, mesh=fine, in_specs=placed, out_specs=P(tm, PAIR, None), check_vma=False
    )
```

```python
import jax
import jax.numpy as jnp
from jax import lax
from jax.experimental import pallas as pl
from jax.experimental.pallas import tpu as pltpu
from jax.sharding import Mesh
from jax.sharding import PartitionSpec as P

NOCC = 128
PAIR = ("zl", "y", "x")
SAME_CORE = ("zh", "zl", "y", "x")
INDEX_ROWS = 8
FIRST = ((0, 1, 2), (3, 1, 2))


def in_hbm(array):
    return pltpu.with_memory_space_constraint(array, pltpu.HBM)


def picked_for(wants, slices):
    owners, rows, cols = slices.shape[0], slices.shape[1] - INDEX_ROWS, slices.shape[2]
    count = 2 * len(FIRST[0])
    per_step = 4

    def kernel(wants_ref, slices_ref, out_ref, sent):
        def some(i, unused):
            for d in range(per_step):
                for half in range(2):
                    for k in range(count):
                        block = wants_ref[i * per_step + d, k % 2, FIRST[half][k // 2]]
                        piece = slices_ref.at[block, pl.ds(0, rows), :]
                        at = out_ref.at[half, i * per_step + d, k]
                        pltpu.make_async_copy(piece, at, sent).start()
            return unused

        lax.fori_loop(0, owners // per_step, some, 0)
        pltpu.make_async_copy(out_ref, out_ref, sent).wait()

    return pl.pallas_call(
        kernel,
        grid_spec=pltpu.PrefetchScalarGridSpec(
            num_scalar_prefetch=1,
            grid=(1,),
            in_specs=[pl.BlockSpec(memory_space=pltpu.VMEM)],
            out_specs=pl.BlockSpec(memory_space=pltpu.HBM),
            scratch_shapes=[pltpu.SemaphoreType.DMA(())],
        ),
        out_shape=pltpu.HBM((2, owners, count, rows, cols), slices.dtype),
        compiler_params=pltpu.CompilerParams(vmem_limit_bytes=16 << 20),
    )(wants, slices)


def pair_sums(where, factors, mine, other, screened, carried):
    _, slots, blocks, rows, cols = mine[0].shape
    parts = len(mine)
    pairs = blocks * parts // 2
    times, _, blk, _ = screened.shape
    norb = factors.shape[-1]
    strip = 256
    last = carried is not None

    def kernel(where_ref, fac, *refs):
        mine_refs, other_refs, refs = refs[:parts], refs[parts : 2 * parts], refs[2 * parts :]
        if last:
            start, tiles, out, left, right, inner, got = refs
        else:
            screened_ref, out, ahead, left, right, inner, tiles, got, seen, moved = refs
        p = pl.program_id(0)
        slot = 0 if last else lax.rem(p, 2)
        own = where_ref[0]

        def bring(q, to):
            for sources, side in ((mine_refs, own), (other_refs, 1 - own)):
                for half in range(2):
                    at = pl.multiple_of((half * 2 + side) * cols, cols)
                    for b, target in enumerate((left, right)):
                        pltpu.make_async_copy(
                            sources[b % parts].at[half, :, (2 * q + b) // parts],
                            target.at[to, :, :, pl.ds(at, cols)],
                            got.at[b, to],
                        ).start()
            if not last:
                for t in range(times):
                    tile(q, t, to).start()

        def tile(q, t, to):
            return pltpu.make_async_copy(
                screened_ref.at[t, where_ref[1 + q]], tiles.at[to, t], seen.at[to, t]
            )

        def later(t):
            return pltpu.make_async_copy(
                screened_ref.at[t, where_ref[1 + pairs]], ahead.at[t], moved.at[t]
            )

        if last:
            bring(0, 0)
        else:

            @pl.when(p == 0)
            def _():
                bring(0, 0)
                for t in range(times):
                    later(t).start()
                out[...] = jnp.zeros(out.shape, out.dtype)

            @pl.when(p + 1 < pairs)
            def _():
                bring(p + 1, 1 - slot)

        for b, target in enumerate((left, right)):
            pltpu.make_async_copy(target.at[slot], target.at[slot], got.at[b, slot]).wait()
        left_side = left[slot].reshape(blk, norb)
        right_side = right[slot].reshape(blk, norb)
        for t in range(times):
            if not last:
                tile(p, t, slot).wait()
            scale = fac[0, t : t + 1, :]
            for s in range(blk // strip):
                part = slice(s * strip, (s + 1) * strip)
                scaled = (left_side[part, :].astype(jnp.float32) * scale).astype(jnp.bfloat16)
                green = lax.dot_general(
                    scaled, right_side, (((1,), (1,)), ((), ())), preferred_element_type=jnp.float32
                )
                held = tiles[t, part, :] if last else tiles[slot, t, part, :]
                product = (green * held.astype(jnp.float32)).astype(jnp.bfloat16)
                inner[t, part, :] = jnp.dot(
                    product, right_side, preferred_element_type=jnp.float32
                ).astype(jnp.bfloat16)
            added = lax.dot_general(
                left_side, inner[t], (((0,), (0,)), ((), ())), preferred_element_type=jnp.float32
            )
            if last:
                total = start[t] + added
                both = (total + total.T).astype(out.dtype)
                out[:, t] = both.reshape(out.shape[0], out.shape[2], norb)
            else:
                out[t] += added

        if not last:

            @pl.when(p == pairs - 1)
            def _():
                for t in range(times):
                    later(t).wait()

    sums = (times, norb, norb)
    here = pl.BlockSpec(memory_space=pltpu.VMEM)
    anywhere = pl.BlockSpec(memory_space=pl.ANY)
    buffers = 1 if last else 2
    scratch = [
        pltpu.VMEM((buffers, slots, rows, norb), jnp.bfloat16),
        pltpu.VMEM((buffers, slots, rows, norb), jnp.bfloat16),
        pltpu.VMEM((times, blk, norb), jnp.bfloat16),
    ]
    if last:
        operands, specs = list(carried), [here, here]
        scratch += [pltpu.SemaphoreType.DMA((2, buffers))]
        out_shape = jax.ShapeDtypeStruct((slots, times, norb // slots, norb), jnp.bfloat16)
        out_specs = here
    else:
        operands, specs = [in_hbm(screened)], [pl.BlockSpec(memory_space=pltpu.HBM)]
        scratch += [
            pltpu.VMEM((buffers, times, blk, blk), jnp.bfloat16),
            pltpu.SemaphoreType.DMA((2, buffers)),
            pltpu.SemaphoreType.DMA((buffers, times)),
            pltpu.SemaphoreType.DMA((times,)),
        ]
        out_shape = (
            jax.ShapeDtypeStruct(sums, jnp.float32),
            jax.ShapeDtypeStruct((times, blk, blk), jnp.bfloat16),
        )
        out_specs = (here, here)
    return pl.pallas_call(
        kernel,
        grid_spec=pltpu.PrefetchScalarGridSpec(
            num_scalar_prefetch=1,
            grid=(pairs,),
            in_specs=[
                pl.BlockSpec((1, times, norb), lambda p, c: (c[1 + p], 0, 0)),
            ]
            + [anywhere] * (2 * parts)
            + specs,
            out_specs=out_specs,
            scratch_shapes=scratch,
        ),
        out_shape=out_shape,
        compiler_params=pltpu.CompilerParams(
            vmem_limit_bytes=40 << 20, dimension_semantics=("arbitrary",)
        ),
    )(where, factors, *mine, *other, *operands)


def shards(orbitals, level_gap, screened, pair_blocks):
    owners = lax.axis_size(PAIR)
    cols = orbitals.shape[1]
    rows = orbitals.shape[0] // owners
    time_local, pair_local = screened.shape[:2]
    norb = level_gap.shape[0]

    asked = jnp.zeros((INDEX_ROWS, cols), jnp.bfloat16)
    asked = asked.at[:2, :pair_local].set(pair_blocks.T.astype(jnp.bfloat16))
    sent = jnp.concatenate(
        [
            orbitals.reshape(owners, rows, cols),
            jnp.broadcast_to(asked, (owners, INDEX_ROWS, cols)),
        ],
        axis=1,
    )
    slices = lax.all_to_all(sent, PAIR, 0, 0, tiled=True)
    wants = slices[:, rows : rows + 2, :pair_local].astype(jnp.int32)

    half = lax.axis_index("zh")
    core = lax.axis_index("core")
    first = jnp.where(half == 0, FIRST[0][0], FIRST[1][0])
    final = jnp.where(half == 0, FIRST[1][0], FIRST[0][0])
    opening = jnp.stack([core, first, FIRST[0][1], FIRST[0][2], final]).astype(jnp.int32)
    closing = jnp.stack([core, final]).astype(jnp.int32)
    swap = [(0, 1), (1, 0)]
    picked = picked_for(wants, slices).reshape(2 * owners, -1, rows, cols)
    mine = lax.all_to_all(picked, SAME_CORE, 0, 0, tiled=True)
    moments = ((half * 2 + core) * time_local + jnp.arange(time_local)).astype(jnp.float32)
    tau = 6.0 * (moments + 0.5) / (time_local * lax.axis_size(("zh", "core")))
    signs = jnp.where(jnp.arange(norb) < NOCC, 1.0, -1.0).astype(jnp.float32)
    weights = jnp.where(pair_blocks[:, 0] == pair_blocks[:, 1], 0.5, 1.0).astype(jnp.float32)
    factors = signs[None, :] * jnp.exp(-level_gap[None, :] * tau[:, None])
    factors = weights[:, None, None] * factors[None]
    other = lax.ppermute(mine, "core", swap)
    traded, twins = [], []
    for b in range(2):
        traded.append(lax.ppermute(mine[:, b : b + 1], "zh", swap))
    shape = (2, owners, -1, rows, cols)
    kept = pair_sums(
        opening, factors, [mine.reshape(shape)], [other.reshape(shape)], screened, None
    )
    for b in range(2):
        twins.append(lax.ppermute(traded[b], "core", swap))
    traded = [part.reshape(shape) for part in traded]
    twins = [part.reshape(shape) for part in twins]
    total = pair_sums(closing, factors, traded, twins, screened, kept)
    shares = lax.all_to_all(total, PAIR, 0, 0, tiled=True)
    return jnp.sum(shares.astype(jnp.float32), axis=0)


def solution(mesh):
    fine = Mesh(mesh.devices.reshape(2, 2, 2, 4, 4), ("zh", "core", "zl", "y", "x"))
    tm = ("zh", "core")
    placed = (P(PAIR, tm), P(), P(tm, PAIR, None, None), P(PAIR, None))
    return jax.shard_map(
        shards, mesh=fine, in_specs=placed, out_specs=P(tm, PAIR, None), check_vma=False
    )
```
